256 devices in a mesh: row: 8 (over x_hi, y), col: 32 (over x_lo, z, core).
Axes of the slice: x: 4 (x_hi: 2, x_lo: 2; x = x_hi * 2 + x_lo), y: 4, z: 8, core: 2. Of those that a mesh axis runs over, the one named last changes fastest.
Arguments:
- forward_op: bfloat16 [12288, 98304], P('row', 'col'), may hold values from -0.01953125 to 0.01953125
- samples: bfloat16 [98304, 256], P('col'), may hold values from -6 to 6
- observed: float32 [256, 12288], P(None, 'row'), may hold values from -9 to 9
- precision: float32 [12288], P('row'), may hold values from 0.3 to 3
Outputs:
- adjoint: float32 [256, 98304], P('row', 'col')
The draws below stay inside these ranges and needn't reach their ends.
All inputs are finite; a program needn't handle non-finite values.
Results may differ from the reference program's by a relative error of at most 0.0028.
Values may be sent and summed in bfloat16 or wider, within the bound.
A program may use at most 64 MiB of HBM per device.

```python
import math
import jax
import jax.numpy as jnp

S = 256
M = 12288
N = 98304


def spiked(result, stream_key, source, target, parts, factor):
    def block_of(dim):
        return (jnp.arange(result.shape[dim]) // (result.shape[dim] // parts)).reshape((-1,) + (1,) * (result.ndim - 1 - dim))

    first = jax.random.permutation(stream_key, parts)[block_of(target)]
    second = (block_of(target) + parts // 2) % parts
    return jnp.where((block_of(source) == first) | (block_of(source) == second), factor * result, result)


def block_levels(key, dims, shards, smallest, high):
    def one(axis_at, parts):
        steps = jax.random.uniform(jax.random.fold_in(jax.random.fold_in(key, 6), axis_at), (parts,), jnp.float32, smallest / len(shards), high / len(shards))
        return jnp.repeat(jnp.exp(steps), dims[axis_at] // parts).reshape((-1,) + (1,) * (len(dims) - axis_at - 1))

    level = one(*shards[0])
    for cut in shards[1:]:
        level = level * one(*cut)
    return level


def centred(key, shape, scale, reach, pieces=(), kind=jnp.bfloat16):
    entries = scale * jax.random.normal(key, shape, jnp.float32)
    if pieces:
        entries = entries * block_levels(key, shape, pieces, -0.22, 0.18)
    return jnp.clip(entries, -reach, reach).astype(kind)


def heavy_noise(key, shape, scale, bound, split, heavy, held_as=jnp.bfloat16):
    result = scale * jax.random.normal(key, shape, jnp.float32)
    if split:
        result = result * block_levels(key, shape, split, -0.22, 0.18)
    return jnp.clip(spiked(result, jax.random.fold_in(key, 3), *heavy), -bound, bound).astype(held_as)


def setup_inputs(seed: int = 0) -> dict:
    key_of = jax.random.split(jax.random.key(seed), 5)
    return {
        "forward_op": centred(key_of[0], (M, N), N ** -0.5, 0.01953125, ((0, 8), (1, 32))),
        "samples": heavy_noise(key_of[1], (N, S), 1.0, 6.0, ((0, 32),), (0, 1, 32, 2.75)),
        "observed": heavy_noise(key_of[2], (S, M), 1.5, 9.0, ((1, 8),), (1, 0, 8, 2.0), jnp.float32),
        "precision": jnp.clip(jnp.exp(math.log(3.0) - 2.3025851 * jax.random.uniform(key_of[3], (M,), jnp.float32) ** block_levels(key_of[3], (M,), ((0, 8),), -0.2, 0.2)), 0.3, 3.0),
    }


dof = 4.0


def student_score(error, precision):
    return (dof + 1.0) * precision * error / (dof + precision * error * error)


def reference(forward_op, samples, observed, precision):
    predicted = jnp.dot(samples.T, forward_op.T, preferred_element_type=jnp.float32)
    scores = student_score(observed - predicted, precision[None, :]).astype(jnp.bfloat16)
    return jnp.dot(scores, forward_op, preferred_element_type=jnp.float32)
```

```python
import jax
import jax.numpy as jnp
from jax import lax
from jax.experimental import pallas as pl
from jax.experimental.pallas import tpu as pltpu
from jax.sharding import PartitionSpec as P

MESH = pl.DeviceIdType.MESH
F32 = jnp.float32
BF16 = jnp.bfloat16

S = 256
MB = 1536
NB = 3072
UNIT = 48
BLK = 384
NC = 256
PAIRS = NB // NC // 2
LAG = 1
TINY = 1e-36
FAR = (4, 3, 5, 2, 6, 1, 7)
NEAR = (1, 7, 2, 6, 3, 5, 4)
dof = 4.0


def enc4(v):
    w = v * v
    return (v * jnp.abs(v) * w).astype(BF16)


def dec4(c):
    v = c.astype(F32)
    t = lax.rsqrt(jnp.maximum(jnp.abs(v), TINY))
    return v * (t * t * lax.rsqrt(t))


def enc2(v):
    return (v * jnp.abs(v)).astype(BF16)


def dec2(c):
    v = c.astype(F32)
    return v * lax.rsqrt(jnp.maximum(jnp.abs(v), TINY))


def student_score(error, precision):
    return (dof + 1.0) * precision * error / (dof + precision * error * error)


def kernel(
    fop_hbm, samp_hbm, obs_hbm, prec_ref, out_ref,
    fop, samp, obs, obs_t, prec_t,
    sib_send, sib_recv, acc, quad, own, x_send, x_recv, z_send, z_recv,
    sc_t, sc, parts, r_send, r_recv, held, h_send, h_recv,
    load_sem, sib_sem, x_sem, z_sem, gz_sem, gx_sem, gs_sem, r_sem, h_sem,
):
    row = lax.axis_index("row")
    col = lax.axis_index("col")
    xh, y = row // 4, row % 4
    xl, z, core = col // 16, (col // 2) % 8, col % 2

    def at_col(x_, z_, c_):
        return (row, x_ * 16 + z_ * 2 + c_)

    sibling = at_col(xl, z, 1 - core)
    xpart = at_col(1 - xl, z, core)
    hpart = ((1 - xh) * 4 + y, col)

    def zpeer(d):
        return at_col(xl, (z + d) % 8, core)

    def ypeer(g):
        return (xh * 4 + (y + g) % 4, col)

    def block_at(c_, x_):
        return pl.multiple_of((c_ * 2 + x_) * BLK, BLK)

    order = ((1 - core, 1 - xl), (1 - core, xl), (core, 1 - xl), (core, xl))
    mine = block_at(core, xl)

    load_samp = pltpu.make_async_copy(samp_hbm, samp, load_sem.at[4])
    load_samp.start()
    load_fop = []
    for j, (c_, x_) in enumerate(order):
        rows = pl.ds(block_at(c_, x_), BLK)
        cp = pltpu.make_async_copy(fop_hbm.at[rows], fop.at[rows], load_sem.at[j])
        cp.start()
        load_fop.append(cp)
    load_obs = pltpu.make_async_copy(obs_hbm.at[:, pl.ds(mine, BLK)], obs, load_sem.at[5])
    load_obs.start()

    barrier = pltpu.get_barrier_semaphore()
    peers = [sibling, xpart, hpart, ypeer(1), ypeer(3)] + [zpeer(d) for d in range(1, 8)]
    for p in peers:
        pl.semaphore_signal(barrier, inc=1, device_id=p, device_id_type=MESH)
    pl.semaphore_wait(barrier, len(peers))

    def remote(src, dst, sems, i, device):
        return pltpu.make_async_remote_copy(
            src_ref=src, dst_ref=dst, send_sem=sems.at[(0,) + i], recv_sem=sems.at[(1,) + i],
            device_id=device, device_id_type=MESH,
        )

    sends = []

    def go(cp):
        cp.start()
        sends.append(cp)
        return cp

    def product(j):
        load_fop[j].wait()
        rows = pl.ds(block_at(*order[j]), BLK)
        return jnp.dot(fop[rows, :], samp[...], preferred_element_type=F32)

    load_samp.wait()
    sib = []
    for j in range(2):
        sib_send[j] = product(j)
        sib.append(go(remote(sib_send.at[j], sib_recv.at[j], sib_sem, (j,), sibling)))
    acc[...] = product(2)
    sib[0].wait_recv()
    xs = {}
    for d in FAR + (0,):
        rows = pl.ds(pl.multiple_of(((z + d) % 8) * UNIT, UNIT), UNIT)
        x_send[d] = enc4(acc[rows, :] + sib_recv[0, rows, :])
        xs[d] = go(remote(x_send.at[d], x_recv.at[d], x_sem, (d,), xpart))
    quad[...] = product(3)
    sib[1].wait_recv()
    zs = {}
    for d in FAR + (0,):
        rows = pl.ds(pl.multiple_of(((z + d) % 8) * UNIT, UNIT), UNIT)
        xs[d].wait_recv()
        v = quad[rows, :] + sib_recv[1, rows, :] + dec4(x_recv[d])
        if d:
            z_send[d] = enc4(v)
            zs[d] = go(remote(z_send.at[d], z_recv.at[d], z_sem, (d,), zpeer(d)))
        else:
            own[...] = v

    load_obs.wait()
    obs_t[...] = obs[...].T
    prec_t[...] = jnp.broadcast_to(prec_ref[:, pl.ds(mine, BLK)], (128, BLK)).T

    pred = own[...]
    for d in NEAR:
        zs[d].wait_recv()
        pred = pred + dec4(z_recv[d])
    rows = pl.ds(pl.multiple_of(z * UNIT, UNIT), UNIT)
    p = prec_t[rows, :]
    p = jnp.concatenate([p, p], axis=1)
    score = student_score(obs_t[rows, :] - pred, p).astype(BF16)

    def unit_at(x_, z_):
        return sc_t.at[pl.ds(pl.multiple_of((core * 2 + x_) * BLK + z_ * UNIT, 16), UNIT)]

    unit_at(xl, z)[...] = score

    def to_x(d):
        zz = (z + 8 - d) % 8
        return remote(unit_at(xl, zz), unit_at(xl, zz), gx_sem, (d,), xpart)

    gx = {0: go(to_x(0))}
    gz = {}
    for d in FAR:
        gz[d] = go(remote(unit_at(xl, z), unit_at(xl, z), gz_sem, (d,), zpeer(d)))
    for d in NEAR:
        gz[d].wait_recv()
        gx[d] = go(to_x(d))

    def to_sibling(k):
        b = sc_t.at[pl.ds(block_at(*order[2 + k]), BLK)]
        return remote(b, b, gs_sem, (k,), sibling)

    def turn(j):
        b = pl.ds(block_at(*order[j]), BLK)
        sc[:, b] = sc_t[b, :].T

    g1 = go(to_sibling(1))
    turn(3)
    for d in (0,) + NEAR:
        gx[d].wait_recv()
    g0 = go(to_sibling(0))
    turn(2)
    g1.wait_recv()
    turn(1)
    g0.wait_recv()
    turn(0)

    def ring(c, s, g):
        return remote(r_send.at[c, s], r_recv.at[c, s], r_sem, (c, s), ypeer(g))

    def far(c):
        return remote(h_send.at[c], h_recv.at[c], h_sem, (c,), hpart)

    def block(c, b):
        lo = parts[c, pl.ds(pl.multiple_of(b * 32, 32), 32), :]
        hi = parts[c, pl.ds(pl.multiple_of(128 + b * 32, 32), 32), :]
        return jnp.concatenate([lo, hi], axis=0)

    def step(t, carry):
        for way, g in enumerate((1, 3)):
            @pl.when(t < PAIRS)
            def _():
                c = 2 * t + way
                columns = pl.ds(pl.multiple_of(c * NC, NC), NC)
                parts[c] = jnp.dot(sc[...], fop[:, columns], preferred_element_type=F32)
                r_send[c, 0] = enc2(block(c, (y + 4 - g) % 4))
                ring(c, 0, g).start()

        for s in (1, 2, 3):
            u = t - s * LAG

            @pl.when((u >= 0) & (u < PAIRS))
            def _():
                for way, g in enumerate((1, 3)):
                    c = 2 * u + way
                    ring(c, s - 1, g).wait_recv()
                    v = dec2(r_recv[c, s - 1]) + block(c, (y + (4 - g) * (s + 1)) % 4)
                    if s < 3:
                        r_send[c, s] = enc2(v)
                        ring(c, s, g).start()
                    else:
                        held[c] = v
                        h_send[c] = enc2(held[c, pl.ds(pl.multiple_of((1 - xh) * 32, 32), 32), :])
                        far(c).start()

        w = t - 4 * LAG

        @pl.when((w >= 0) & (w < PAIRS))
        def _():
            for way in range(2):
                c = 2 * w + way
                columns = pl.ds(pl.multiple_of(c * NC, NC), NC)
                far(c).wait_recv()
                out_ref[:, columns] = held[c, pl.ds(pl.multiple_of(xh * 32, 32), 32), :] + dec2(h_recv[c])

        return carry

    lax.fori_loop(0, PAIRS + 4 * LAG, step, 0)

    for cp in sends:
        cp.wait_send()

    def drain(t, carry):
        for way, g in enumerate((1, 3)):
            c = 2 * t + way
            for s in range(3):
                ring(c, s, g).wait_send()
            far(c).wait_send()
        return carry

    lax.fori_loop(0, PAIRS, drain, 0)


def local(forward_op, samples, observed, precision):
    chunks = NB // NC
    dma = pltpu.SemaphoreType.DMA
    return pl.pallas_call(
        kernel,
        out_shape=jax.ShapeDtypeStruct((S // 8, NB), F32),
        in_specs=[pl.BlockSpec(memory_space=pltpu.HBM)] * 3 + [pl.BlockSpec(memory_space=pltpu.VMEM)],
        out_specs=pl.BlockSpec(memory_space=pltpu.VMEM),
        scratch_shapes=[
            pltpu.VMEM((MB, NB), BF16),
            pltpu.VMEM((NB, S), BF16),
            pltpu.VMEM((S, BLK), F32),
            pltpu.VMEM((BLK, S), F32),
            pltpu.VMEM((BLK, 128), F32),
            pltpu.VMEM((2, BLK, S), F32),
            pltpu.VMEM((2, BLK, S), F32),
            pltpu.VMEM((BLK, S), F32),
            pltpu.VMEM((BLK, S), F32),
            pltpu.VMEM((UNIT, S), F32),
            pltpu.VMEM((8, UNIT, S), BF16),
            pltpu.VMEM((8, UNIT, S), BF16),
            pltpu.VMEM((8, UNIT, S), BF16),
            pltpu.VMEM((8, UNIT, S), BF16),
            pltpu.VMEM((MB, S), BF16),
            pltpu.VMEM((S, MB), BF16),
            pltpu.VMEM((chunks, S, NC), F32),
            pltpu.VMEM((chunks, 3, 64, NC), BF16),
            pltpu.VMEM((chunks, 3, 64, NC), BF16),
            pltpu.VMEM((chunks, 64, NC), F32),
            pltpu.VMEM((chunks, 32, NC), BF16),
            pltpu.VMEM((chunks, 32, NC), BF16),
            dma((6,)),
            dma((2, 2)),
            dma((2, 8)),
            dma((2, 8)),
            dma((2, 8)),
            dma((2, 8)),
            dma((2, 2)),
            dma((2, chunks, 3)),
            dma((2, chunks)),
        ],
        compiler_params=pltpu.CompilerParams(
            collective_id=0, has_side_effects=True, vmem_limit_bytes=48 * 1024 * 1024
        ),
    )(forward_op, samples, observed, precision.reshape(1, MB))


def solution(mesh):
    return jax.shard_map(
        local,
        mesh=mesh,
        in_specs=(P("row", "col"), P("col", None), P(None, "row"), P("row")),
        out_specs=P("row", "col"),
        check_vma=False,
    )
```

```python
import jax
import jax.numpy as jnp
from jax import lax
from jax.experimental import pallas as pl
from jax.experimental.pallas import tpu as pltpu
from jax.sharding import PartitionSpec as P

MESH = pl.DeviceIdType.MESH
F32 = jnp.float32
BF16 = jnp.bfloat16

S = 256
MB = 1536
NB = 3072
UNIT = 48
BLK = 384
NC = 256
CHUNKS = NB // NC
YF = 5
XF = CHUNKS - YF
TINY = 1e-36
FAR = (4, 3, 5, 2, 6, 1, 7)
NEAR = (1, 7, 2, 6, 3, 5, 4)
dof = 4.0


def enc4(v):
    w = v * v
    return (v * jnp.abs(v) * w).astype(BF16)


def dec4(c):
    v = c.astype(F32)
    t = lax.rsqrt(jnp.maximum(jnp.abs(v), TINY))
    return v * (t * t * lax.rsqrt(t))


def enc2(v):
    return (v * jnp.abs(v)).astype(BF16)


def dec2(c):
    v = c.astype(F32)
    return v * lax.rsqrt(jnp.maximum(jnp.abs(v), TINY))


def student_score(error, precision):
    return (dof + 1.0) * precision * error / (dof + precision * error * error)


def kernel(
    fop_hbm, samp_hbm, obs_hbm, prec_hbm, out_ref,
    fop, samp, obs, prec, obs_t, prec_t,
    sib_send, sib_recv, acc, quad, own, x_send, x_recv, z_send, z_recv,
    sc_t, sc, parts, held, xx_send, xx_recv, xy_send, xy_recv, yy_send, yy_recv, yx_send, yx_recv,
    load_sem, sib_sem, x_sem, z_sem, gz_sem, gx_sem, gs_sem, xx_sem, xy_sem, yy_sem, yx_sem,
):
    row = lax.axis_index("row")
    col = lax.axis_index("col")
    xh, y = row // 4, row % 4
    xl, z, core = col // 16, (col // 2) % 8, col % 2

    def at_col(x_, z_, c_):
        return (row, x_ * 16 + z_ * 2 + c_)

    sibling = at_col(xl, z, 1 - core)
    xpart = at_col(1 - xl, z, core)
    hpart = ((1 - xh) * 4 + y, col)

    def zpeer(d):
        return at_col(xl, (z + d) % 8, core)

    def ypeer(d):
        return (xh * 4 + (y + d) % 4, col)

    def block_at(c_, x_):
        return pl.multiple_of((c_ * 2 + x_) * BLK, BLK)

    order = ((1 - core, 1 - xl), (core, 1 - xl), (1 - core, xl), (core, xl))
    mine = block_at(core, xl)

    load_samp = pltpu.make_async_copy(samp_hbm, samp, load_sem.at[4])
    load_samp.start()
    load_fop = []
    for j, (c_, x_) in enumerate(order):
        rows = pl.ds(block_at(c_, x_), BLK)
        cp = pltpu.make_async_copy(fop_hbm.at[rows], fop.at[rows], load_sem.at[j])
        cp.start()
        load_fop.append(cp)
    load_obs = pltpu.make_async_copy(obs_hbm.at[:, pl.ds(mine, BLK)], obs, load_sem.at[5])
    load_obs.start()
    load_prec = pltpu.make_async_copy(prec_hbm, prec, load_sem.at[6])
    load_prec.start()

    barrier = pltpu.get_barrier_semaphore()
    peers = [sibling, xpart, hpart, ypeer(1), ypeer(2), ypeer(3)] + [zpeer(d) for d in range(1, 8)]
    for p in peers:
        pl.semaphore_signal(barrier, inc=1, device_id=p, device_id_type=MESH)
    pl.semaphore_wait(barrier, len(peers))

    def remote(src, dst, sems, i, device):
        return pltpu.make_async_remote_copy(
            src_ref=src, dst_ref=dst, send_sem=sems.at[(0,) + i], recv_sem=sems.at[(1,) + i],
            device_id=device, device_id_type=MESH,
        )

    sends = []

    def go(cp):
        cp.start()
        sends.append(cp)
        return cp

    def product(j):
        load_fop[j].wait()
        rows = pl.ds(block_at(*order[j]), BLK)
        return jnp.dot(fop[rows, :], samp[...], preferred_element_type=F32)

    load_samp.wait()
    sib_send[0] = product(0)
    sib0 = go(remote(sib_send.at[0], sib_recv.at[0], sib_sem, (0,), sibling))
    acc[...] = product(1)
    sib0.wait_recv()
    xs = {}
    for d in FAR + (0,):
        rows = pl.ds(pl.multiple_of(((z + d) % 8) * UNIT, UNIT), UNIT)
        x_send[d] = enc4(acc[rows, :] + sib_recv[0, rows, :])
        xs[d] = go(remote(x_send.at[d], x_recv.at[d], x_sem, (d,), xpart))
    sib_send[1] = product(2)
    sib1 = go(remote(sib_send.at[1], sib_recv.at[1], sib_sem, (1,), sibling))
    quad[...] = product(3)
    sib1.wait_recv()
    zs = {}
    for d in FAR + (0,):
        rows = pl.ds(pl.multiple_of(((z + d) % 8) * UNIT, UNIT), UNIT)
        xs[d].wait_recv()
        v = quad[rows, :] + sib_recv[1, rows, :] + dec4(x_recv[d])
        if d:
            z_send[d] = enc4(v)
            zs[d] = go(remote(z_send.at[d], z_recv.at[d], z_sem, (d,), zpeer(d)))
        else:
            own[...] = v

    load_obs.wait()
    load_prec.wait()
    obs_t[...] = obs[...].T
    prec_t[...] = jnp.broadcast_to(prec[pl.ds(mine, BLK)].reshape(1, BLK), (128, BLK)).T

    pred = own[...]
    for d in NEAR:
        zs[d].wait_recv()
        pred = pred + dec4(z_recv[d])
    rows = pl.ds(pl.multiple_of(z * UNIT, UNIT), UNIT)
    p = prec_t[rows, :]
    p = jnp.concatenate([p, p], axis=1)
    score = student_score(obs_t[rows, :] - pred, p).astype(BF16)

    def unit_at(x_, z_):
        return sc_t.at[pl.ds(pl.multiple_of((core * 2 + x_) * BLK + z_ * UNIT, 16), UNIT)]

    unit_at(xl, z)[...] = score

    def to_x(d):
        zz = (z + 8 - d) % 8
        return remote(unit_at(xl, zz), unit_at(xl, zz), gx_sem, (d,), xpart)

    gx = {0: go(to_x(0))}
    gz = {}
    for d in NEAR:
        gz[d] = go(remote(unit_at(xl, z), unit_at(xl, z), gz_sem, (d,), zpeer(d)))
    for d in NEAR:
        gz[d].wait_recv()
        gx[d] = go(to_x(d))

    def to_sibling(k):
        b = sc_t.at[pl.ds(block_at(core, (1 - xl, xl)[k]), BLK)]
        return remote(b, b, gs_sem, (k,), sibling)

    def turn(j):
        b = pl.ds(block_at(*order[j]), BLK)
        sc[:, b] = sc_t[b, :].T

    g1 = go(to_sibling(1))
    turn(3)
    for d in (0,) + NEAR:
        gx[d].wait_recv()
    g0 = go(to_sibling(0))
    turn(1)
    g1.wait_recv()
    turn(2)
    g0.wait_recv()
    turn(0)

    def columns(c):
        return pl.ds(pl.multiple_of(c * NC, NC), NC)

    def dest(x_, y_):
        return pl.ds(pl.multiple_of(x_ * 128 + y_ * 32, 32), 32)

    def half(x_):
        return pl.ds(pl.multiple_of(x_ * 128, 128), 128)

    def xx(i):
        return remote(xx_send.at[i], xx_recv.at[i], xx_sem, (i,), hpart)

    def xy(i, d):
        return remote(xy_send.at[i, d - 1], xy_recv.at[i, d - 1], xy_sem, (i, d - 1), ypeer(d))

    def yy(j, d):
        return remote(yy_send.at[j, d - 1], yy_recv.at[j, d - 1], yy_sem, (j, d - 1), ypeer(d))

    def yx(j):
        return remote(yx_send.at[j], yx_recv.at[j], yx_sem, (j,), hpart)

    def adjoint(c):
        parts[c] = jnp.dot(sc[...], fop[:, columns(c)], preferred_element_type=F32)

    def x_first(i, c):
        adjoint(c)
        xx_send[i] = enc2(parts[c, half(1 - xh), :])
        xx(i).start()

    def y_first(j, c):
        adjoint(c)
        for d in (2, 1, 3):
            y_ = (y + d) % 4
            yy_send[j, d - 1, :32] = enc2(parts[c, dest(0, y_), :])
            yy_send[j, d - 1, 32:] = enc2(parts[c, dest(1, y_), :])
            yy(j, d).start()

    def x_then_y(i, c):
        xx(i).wait_recv()
        for d in (2, 1, 3, 0):
            y_ = (y + d) % 4
            v = parts[c, dest(xh, y_), :] + dec2(xx_recv[i, pl.ds(pl.multiple_of(y_ * 32, 32), 32), :])
            if d:
                xy_send[i, d - 1] = enc2(v)
                xy(i, d).start()
            else:
                held[c] = v

    def y_then_x(j, c):
        for d in (1, 3, 2):
            yy(j, d).wait_recv()

        def total(x_):
            v = parts[c, dest(x_, y), :]
            for d in (1, 2, 3):
                v = v + dec2(yy_recv[j, d - 1, pl.ds(pl.multiple_of(x_ * 32, 32), 32), :])
            return v

        yx_send[j] = enc2(total(1 - xh))
        yx(j).start()
        held[c] = total(xh)

    def end_x_first(i, c):
        v = held[c]
        for d in (1, 3, 2):
            xy(i, d).wait_recv()
            v = v + dec2(xy_recv[i, d - 1])
        out_ref[:, columns(c)] = v

    def end_y_first(j, c):
        yx(j).wait_recv()
        out_ref[:, columns(c)] = held[c] + dec2(yx_recv[j])

    def drain_x(i, c):
        xx(i).wait_send()
        for d in (1, 2, 3):
            xy(i, d).wait_send()

    def drain_y(j, c):
        yx(j).wait_send()
        for d in (1, 2, 3):
            yy(j, d).wait_send()

    def sweep(on_x, on_y):
        def both(t, carry):
            on_x(t, 2 * t)
            on_y(t, 2 * t + 1)
            return carry

        def rest(t, carry):
            on_x(t, t + YF)
            return carry

        lax.fori_loop(0, YF, both, 0)
        lax.fori_loop(YF, XF, rest, 0)

    sweep(x_first, y_first)
    sweep(x_then_y, y_then_x)
    sweep(end_x_first, end_y_first)
    for cp in sends:
        cp.wait_send()
    sweep(drain_x, drain_y)


def local(forward_op, samples, observed, precision):
    dma = pltpu.SemaphoreType.DMA
    return pl.pallas_call(
        kernel,
        out_shape=jax.ShapeDtypeStruct((S // 8, NB), F32),
        in_specs=[pl.BlockSpec(memory_space=pltpu.HBM)] * 4,
        out_specs=pl.BlockSpec(memory_space=pltpu.VMEM),
        scratch_shapes=[
            pltpu.VMEM((MB, NB), BF16),
            pltpu.VMEM((NB, S), BF16),
            pltpu.VMEM((S, BLK), F32),
            pltpu.VMEM((MB,), F32),
            pltpu.VMEM((BLK, S), F32),
            pltpu.VMEM((BLK, 128), F32),
            pltpu.VMEM((2, BLK, S), F32),
            pltpu.VMEM((2, BLK, S), F32),
            pltpu.VMEM((BLK, S), F32),
            pltpu.VMEM((BLK, S), F32),
            pltpu.VMEM((UNIT, S), F32),
            pltpu.VMEM((8, UNIT, S), BF16),
            pltpu.VMEM((8, UNIT, S), BF16),
            pltpu.VMEM((8, UNIT, S), BF16),
            pltpu.VMEM((8, UNIT, S), BF16),
            pltpu.VMEM((MB, S), BF16),
            pltpu.VMEM((S, MB), BF16),
            pltpu.VMEM((CHUNKS, S, NC), F32),
            pltpu.VMEM((CHUNKS, 32, NC), F32),
            pltpu.VMEM((XF, 128, NC), BF16),
            pltpu.VMEM((XF, 128, NC), BF16),
            pltpu.VMEM((XF, 3, 32, NC), BF16),
            pltpu.VMEM((XF, 3, 32, NC), BF16),
            pltpu.VMEM((YF, 3, 64, NC), BF16),
            pltpu.VMEM((YF, 3, 64, NC), BF16),
            pltpu.VMEM((YF, 32, NC), BF16),
            pltpu.VMEM((YF, 32, NC), BF16),
            dma((7,)),
            dma((2, 2)),
            dma((2, 8)),
            dma((2, 8)),
            dma((2, 8)),
            dma((2, 8)),
            dma((2, 2)),
            dma((2, XF)),
            dma((2, XF, 3)),
            dma((2, YF, 3)),
            dma((2, YF)),
        ],
        compiler_params=pltpu.CompilerParams(
            collective_id=0, has_side_effects=True, vmem_limit_bytes=48 * 1024 * 1024
        ),
    )(*[pltpu.with_memory_space_constraint(a, pltpu.HBM) for a in (forward_op, samples, observed, precision)])


def solution(mesh):
    return jax.shard_map(
        local,
        mesh=mesh,
        in_specs=(P("row", "col"), P("col", None), P(None, "row"), P("row")),
        out_specs=P("row", "col"),
        check_vma=False,
    )
```

```python
import jax
import jax.numpy as jnp
from jax import lax
from jax.experimental import pallas as pl
from jax.experimental.pallas import tpu as pltpu
from jax.sharding import PartitionSpec as P

MESH = pl.DeviceIdType.MESH
F32 = jnp.float32
BF16 = jnp.bfloat16

S = 256
MB = 1536
NB = 3072
UNIT = 48
BLK = 384
NC = 256
CHUNKS = NB // NC
YF = 6
XF = CHUNKS - YF
TINY = 1e-36
FAR = (4, 3, 5, 2, 6, 1, 7)
NEAR = (1, 7, 2, 6, 3, 5, 4)
RDIRECT = ()
GDIRECT = (1, 7, 2, 6)
dof = 4.0


def enc4(v):
    w = v * v
    return (v * jnp.abs(v) * w).astype(BF16)


def dec4(c):
    v = c.astype(F32)
    t = lax.rsqrt(jnp.maximum(jnp.abs(v), TINY))
    return v * (t * t * lax.rsqrt(t))


def enc2(v):
    return (v * jnp.abs(v)).astype(BF16)


def dec2(c):
    v = c.astype(F32)
    return v * lax.rsqrt(jnp.maximum(jnp.abs(v), TINY))


def student_score(error, precision):
    return (dof + 1.0) * precision * error / (dof + precision * error * error)


def kernel(
    fop_hbm, samp_hbm, obs_hbm, prec_hbm, out_ref,
    fop, samp, obs, prec, obs_t, prec_t,
    sib_send, sib_recv, acc, quad, x_send, x_recv, z_send, z_recv, zx_recv,
    sc_t, sc, parts, held, xx_send, xx_recv, xy_send, xy_recv, yy_send, yy_recv, yx_send, yx_recv,
    load_sem, sib_sem, x_sem, z_sem, zx_sem, gz_sem, gx_sem, gs_sem, xx_sem, xy_sem, yy_sem, yx_sem,
):
    row = lax.axis_index("row")
    col = lax.axis_index("col")
    xh, y = row // 4, row % 4
    xl, z, core = col // 16, (col // 2) % 8, col % 2

    def at_col(x_, z_, c_):
        return (row, x_ * 16 + z_ * 2 + c_)

    sibling = at_col(xl, z, 1 - core)
    xpart = at_col(1 - xl, z, core)
    hpart = ((1 - xh) * 4 + y, col)

    def zpeer(d):
        return at_col(xl, (z + d) % 8, core)

    def across(d):
        return at_col(1 - xl, (z + d) % 8, core)

    def ypeer(d):
        return (xh * 4 + (y + d) % 4, col)

    def block_at(c_, x_):
        return pl.multiple_of((c_ * 2 + x_) * BLK, BLK)

    order = ((1 - core, 1 - xl), (core, 1 - xl), (1 - core, xl), (core, xl))
    mine = block_at(core, xl)

    load_samp = pltpu.make_async_copy(samp_hbm, samp, load_sem.at[4])
    load_fop = []
    for j, (c_, x_) in enumerate(order):
        rows = pl.ds(block_at(c_, x_), BLK)
        load_fop.append(pltpu.make_async_copy(fop_hbm.at[rows], fop.at[rows], load_sem.at[j]))
    load_obs = pltpu.make_async_copy(obs_hbm.at[:, pl.ds(mine, BLK)], obs, load_sem.at[5])
    load_prec = pltpu.make_async_copy(prec_hbm, prec, load_sem.at[6])
    load_samp.start()
    load_fop[0].start()

    barrier = pltpu.get_barrier_semaphore()
    peers = [sibling, xpart, hpart, ypeer(1), ypeer(2), ypeer(3)] + [zpeer(d) for d in range(1, 8)]
    peers += [across(d) for d in sorted(set(RDIRECT + GDIRECT))]
    for p in peers:
        pl.semaphore_signal(barrier, inc=1, device_id=p, device_id_type=MESH)

    def remote(src, dst, sems, i, device):
        return pltpu.make_async_remote_copy(
            src_ref=src, dst_ref=dst, send_sem=sems.at[(0,) + i], recv_sem=sems.at[(1,) + i],
            device_id=device, device_id_type=MESH,
        )

    sends = []

    def go(cp):
        cp.start()
        sends.append(cp)
        return cp

    def product(j):
        load_fop[j].wait()
        if j < 2:
            load_fop[j + 2].start()
        if j == 1:
            load_obs.start()
            load_prec.start()
        rows = pl.ds(block_at(*order[j]), BLK)
        return jnp.dot(fop[rows, :], samp[...], preferred_element_type=F32)

    load_samp.wait()
    load_fop[1].start()
    sib_send[0] = product(0)
    pl.semaphore_wait(barrier, len(peers))
    sib0 = go(remote(sib_send.at[0], sib_recv.at[0], sib_sem, (0,), sibling))
    acc[...] = product(1)
    sib0.wait_recv()

    def piece(d):
        return pl.ds(pl.multiple_of(((z + d) % 8) * UNIT, UNIT), UNIT)

    relay = tuple(d for d in FAR if d not in RDIRECT)
    xs, zs, zxs = {}, {}, {}
    for d in relay + RDIRECT + (0,):
        x_send[d] = enc4(acc[piece(d), :] + sib_recv[0, piece(d), :])
        if d in RDIRECT:
            zxs[d] = go(remote(x_send.at[d], zx_recv.at[d], zx_sem, (d,), across(d)))
        else:
            xs[d] = go(remote(x_send.at[d], x_recv.at[d], x_sem, (d,), xpart))
    sib_send[1] = product(2)
    sib1 = go(remote(sib_send.at[1], sib_recv.at[1], sib_sem, (1,), sibling))
    quad[...] = product(3)
    sib1.wait_recv()
    quad[...] = quad[...] + sib_recv[1]
    for d in RDIRECT + relay:
        v = quad[piece(d), :]
        if d in relay:
            xs[d].wait_recv()
            v = v + dec4(x_recv[d])
        z_send[d] = enc4(v)
        zs[d] = go(remote(z_send.at[d], z_recv.at[d], z_sem, (d,), zpeer(d)))

    load_obs.wait()
    load_prec.wait()
    obs_t[...] = obs[...].T
    prec_t[...] = jnp.broadcast_to(prec[pl.ds(mine, BLK)].reshape(1, BLK), (128, BLK)).T

    pred = quad[piece(0), :]
    for d in RDIRECT:
        zs[d].wait_recv()
        pred = pred + dec4(z_recv[d])
    for d in relay:
        zs[d].wait_recv()
        pred = pred + dec4(z_recv[d])
    for d in RDIRECT:
        zxs[d].wait_recv()
        pred = pred + dec4(zx_recv[d])
    xs[0].wait_recv()
    pred = pred + dec4(x_recv[0])
    rows = pl.ds(pl.multiple_of(z * UNIT, UNIT), UNIT)
    p = prec_t[rows, :]
    p = jnp.concatenate([p, p], axis=1)
    score = student_score(obs_t[rows, :] - pred, p).astype(BF16)

    def unit_at(x_, z_):
        return sc_t.at[pl.ds(pl.multiple_of((core * 2 + x_) * BLK + z_ * UNIT, 16), UNIT)]

    unit_at(xl, z)[...] = score

    def to_x(d):
        zz = (z + 8 - d) % 8
        return remote(unit_at(xl, zz), unit_at(xl, zz), gx_sem, (d,), xpart)

    def direct(d):
        return remote(unit_at(xl, z), unit_at(xl, z), gx_sem, (d,), across(d))

    pass_on = tuple(d for d in FAR if d not in GDIRECT)
    gz, gx = {}, {}
    gx[0] = go(to_x(0))
    for d in pass_on + GDIRECT:
        gz[d] = go(remote(unit_at(xl, z), unit_at(xl, z), gz_sem, (d,), zpeer(d)))
    for d in GDIRECT:
        gx[d] = go(direct(d))
    for d in pass_on:
        gz[d].wait_recv()
        gx[d] = go(to_x(d))
    for d in GDIRECT:
        gz[d].wait_recv()

    def to_sibling(k):
        b = sc_t.at[pl.ds(block_at(core, (1 - xl, xl)[k]), BLK)]
        return remote(b, b, gs_sem, (k,), sibling)

    def turn(j):
        b = pl.ds(block_at(*order[j]), BLK)
        sc[:, b] = sc_t[b, :].T

    g1 = go(to_sibling(1))
    turn(3)
    for d in (0,) + GDIRECT + pass_on:
        gx[d].wait_recv()
    g0 = go(to_sibling(0))
    turn(1)
    g1.wait_recv()
    turn(2)
    g0.wait_recv()
    turn(0)

    def columns(c):
        return pl.ds(pl.multiple_of(c * NC, NC), NC)

    def dest(x_, y_):
        return pl.ds(pl.multiple_of(x_ * 128 + y_ * 32, 32), 32)

    def half(x_):
        return pl.ds(pl.multiple_of(x_ * 128, 128), 128)

    def xx(i):
        return remote(xx_send.at[i], xx_recv.at[i], xx_sem, (i,), hpart)

    def xy(i, d):
        return remote(xy_send.at[i, d - 1], xy_recv.at[i, d - 1], xy_sem, (i, d - 1), ypeer(d))

    def yy(j, d):
        return remote(yy_send.at[j, d - 1], yy_recv.at[j, d - 1], yy_sem, (j, d - 1), ypeer(d))

    def yx(j):
        return remote(yx_send.at[j], yx_recv.at[j], yx_sem, (j,), hpart)

    def adjoint(c):
        parts[c] = jnp.dot(sc[...], fop[:, columns(c)], preferred_element_type=F32)

    def x_first(i, c):
        adjoint(c)
        xx_send[i] = enc2(parts[c, half(1 - xh), :])
        xx(i).start()

    def y_first(j, c):
        adjoint(c)
        for d in (2, 1, 3):
            y_ = (y + d) % 4
            yy_send[j, d - 1, :32] = enc2(parts[c, dest(0, y_), :])
            yy_send[j, d - 1, 32:] = enc2(parts[c, dest(1, y_), :])
            yy(j, d).start()

    def x_then_y(i, c):
        xx(i).wait_recv()
        for d in (2, 1, 3, 0):
            y_ = (y + d) % 4
            v = parts[c, dest(xh, y_), :] + dec2(xx_recv[i, pl.ds(pl.multiple_of(y_ * 32, 32), 32), :])
            if d:
                xy_send[i, d - 1] = enc2(v)
                xy(i, d).start()
            else:
                held[c] = v

    def y_then_x(j, c):
        for d in (1, 3, 2):
            yy(j, d).wait_recv()

        def total(x_):
            v = parts[c, dest(x_, y), :]
            for d in (1, 2, 3):
                v = v + dec2(yy_recv[j, d - 1, pl.ds(pl.multiple_of(x_ * 32, 32), 32), :])
            return v

        yx_send[j] = enc2(total(1 - xh))
        yx(j).start()
        held[c] = total(xh)

    def end_x_first(i, c):
        v = held[c]
        for d in (1, 3, 2):
            xy(i, d).wait_recv()
            v = v + dec2(xy_recv[i, d - 1])
        out_ref[:, columns(c)] = v

    def end_y_first(j, c):
        yx(j).wait_recv()
        out_ref[:, columns(c)] = held[c] + dec2(yx_recv[j])

    def drain_x(i, c):
        xx(i).wait_send()
        for d in (1, 2, 3):
            xy(i, d).wait_send()

    def drain_y(j, c):
        yx(j).wait_send()
        for d in (1, 2, 3):
            yy(j, d).wait_send()

    def sweep(on_x, on_y):
        def both(t, carry):
            on_x(t, 2 * t)
            on_y(t, 2 * t + 1)
            return carry

        def rest(t, carry):
            on_x(t, t + YF)
            return carry

        lax.fori_loop(0, YF, both, 0)
        lax.fori_loop(YF, XF, rest, 0)

    sweep(x_first, y_first)
    sweep(x_then_y, y_then_x)
    sweep(end_x_first, end_y_first)
    for cp in sends:
        cp.wait_send()
    sweep(drain_x, drain_y)


def local(forward_op, samples, observed, precision):
    dma = pltpu.SemaphoreType.DMA
    return pl.pallas_call(
        kernel,
        out_shape=jax.ShapeDtypeStruct((S // 8, NB), F32),
        in_specs=[pl.BlockSpec(memory_space=pltpu.HBM)] * 4,
        out_specs=pl.BlockSpec(memory_space=pltpu.VMEM),
        scratch_shapes=[
            pltpu.VMEM((MB, NB), BF16),
            pltpu.VMEM((NB, S), BF16),
            pltpu.VMEM((S, BLK), F32),
            pltpu.VMEM((MB,), F32),
            pltpu.VMEM((BLK, S), F32),
            pltpu.VMEM((BLK, 128), F32),
            pltpu.VMEM((2, BLK, S), F32),
            pltpu.VMEM((2, BLK, S), F32),
            pltpu.VMEM((BLK, S), F32),
            pltpu.VMEM((BLK, S), F32),
            pltpu.VMEM((8, UNIT, S), BF16),
            pltpu.VMEM((8, UNIT, S), BF16),
            pltpu.VMEM((8, UNIT, S), BF16),
            pltpu.VMEM((8, UNIT, S), BF16),
            pltpu.VMEM((8, UNIT, S), BF16),
            pltpu.VMEM((MB, S), BF16),
            pltpu.VMEM((S, MB), BF16),
            pltpu.VMEM((CHUNKS, S, NC), F32),
            pltpu.VMEM((CHUNKS, 32, NC), F32),
            pltpu.VMEM((XF, 128, NC), BF16),
            pltpu.VMEM((XF, 128, NC), BF16),
            pltpu.VMEM((XF, 3, 32, NC), BF16),
            pltpu.VMEM((XF, 3, 32, NC), BF16),
            pltpu.VMEM((YF, 3, 64, NC), BF16),
            pltpu.VMEM((YF, 3, 64, NC), BF16),
            pltpu.VMEM((YF, 32, NC), BF16),
            pltpu.VMEM((YF, 32, NC), BF16),
            dma((7,)),
            dma((2, 2)),
            dma((2, 8)),
            dma((2, 8)),
            dma((2, 8)),
            dma((2, 8)),
            dma((2, 8)),
            dma((2, 2)),
            dma((2, XF)),
            dma((2, XF, 3)),
            dma((2, YF, 3)),
            dma((2, YF)),
        ],
        compiler_params=pltpu.CompilerParams(
            collective_id=0, has_side_effects=True, vmem_limit_bytes=48 * 1024 * 1024
        ),
    )(*[pltpu.with_memory_space_constraint(a, pltpu.HBM) for a in (forward_op, samples, observed, precision)])


def solution(mesh):
    return jax.shard_map(
        local,
        mesh=mesh,
        in_specs=(P("row", "col"), P("col", None), P(None, "row"), P("row")),
        out_specs=P("row", "col"),
        check_vma=False,
    )
```

```python
import jax
import jax.numpy as jnp
from jax import lax
from jax.experimental import pallas as pl
from jax.experimental.pallas import tpu as pltpu
from jax.sharding import PartitionSpec as P

MESH = pl.DeviceIdType.MESH
F32 = jnp.float32
BF16 = jnp.bfloat16

S = 256
MB = 1536
NB = 3072
UNIT = 48
BLK = 384
NC = 256
CHUNKS = NB // NC
YF = 6
XF = CHUNKS - YF
HALF = 128
EARLY = 2
TINY = 1e-36
FAR = (4, 3, 5, 2, 6, 1, 7)
DIRECT = (1, 7, 2, 6)
RELAY = (4, 3, 5)
dof = 4.0


def enc4(v):
    w = v * v
    return (v * jnp.abs(v) * w).astype(BF16)


def dec4(c):
    v = c.astype(F32)
    t = lax.rsqrt(jnp.maximum(jnp.abs(v), TINY))
    return v * (t * t * lax.rsqrt(t))


def enc2(v):
    return (v * jnp.abs(v)).astype(BF16)


def dec2(c):
    v = c.astype(F32)
    return v * lax.rsqrt(jnp.maximum(jnp.abs(v), TINY))


def student_score(error, precision):
    return (dof + 1.0) * precision * error / (dof + precision * error * error)


def kernel(
    fop_hbm, samp_hbm, obs_hbm, prec_hbm, out_ref,
    fop, samp, obs, prec, obs_t, prec_t,
    sib_send, sib_recv, acc, quad, x_send, x_recv, z_send, z_recv,
    sc_t, sc, parts, held, xx_send, xx_recv, xy_send, xy_recv, yy_send, yy_recv, yx_send, yx_recv,
    load_sem, sib_sem, x_sem, z_sem, gz_sem, gx_sem, gs_sem, xx_sem, xy_sem, yy_sem, yx_sem,
):
    row = lax.axis_index("row")
    col = lax.axis_index("col")
    xh, y = row // 4, row % 4
    xl, z, core = col // 16, (col // 2) % 8, col % 2

    def at_col(x_, z_, c_):
        return (row, x_ * 16 + z_ * 2 + c_)

    sibling = at_col(xl, z, 1 - core)
    xpart = at_col(1 - xl, z, core)
    hpart = ((1 - xh) * 4 + y, col)

    def zpeer(d):
        return at_col(xl, (z + d) % 8, core)

    def across(d):
        return at_col(1 - xl, (z + d) % 8, core)

    def ypeer(d):
        return (xh * 4 + (y + d) % 4, col)

    def block_at(c_, x_):
        return pl.multiple_of((c_ * 2 + x_) * BLK, BLK)

    order = ((1 - core, 1 - xl), (core, 1 - xl), (1 - core, xl), (core, xl))
    mine = block_at(core, xl)

    load_samp = pltpu.make_async_copy(samp_hbm, samp, load_sem.at[4])
    load_fop = []
    for j, (c_, x_) in enumerate(order):
        rows = pl.ds(block_at(c_, x_), BLK)
        load_fop.append(pltpu.make_async_copy(fop_hbm.at[rows], fop.at[rows], load_sem.at[j]))
    load_obs = pltpu.make_async_copy(obs_hbm.at[:, pl.ds(mine, BLK)], obs, load_sem.at[5])
    load_prec = pltpu.make_async_copy(prec_hbm, prec, load_sem.at[6])
    load_samp.start()
    load_fop[0].start()

    barrier = pltpu.get_barrier_semaphore()
    peers = [sibling, xpart, hpart, ypeer(1), ypeer(2), ypeer(3)] + [zpeer(d) for d in range(1, 8)]
    peers += [across(d) for d in DIRECT]
    for p in peers:
        pl.semaphore_signal(barrier, inc=1, device_id=p, device_id_type=MESH)

    def remote(src, dst, sems, i, device):
        return pltpu.make_async_remote_copy(
            src_ref=src, dst_ref=dst, send_sem=sems.at[(0,) + i], recv_sem=sems.at[(1,) + i],
            device_id=device, device_id_type=MESH,
        )

    sends = []

    def go(cp):
        cp.start()
        sends.append(cp)
        return cp

    def product(j):
        load_fop[j].wait()
        if j < 2:
            load_fop[j + 2].start()
        if j == 1:
            load_obs.start()
            load_prec.start()
        rows = pl.ds(block_at(*order[j]), BLK)
        return jnp.dot(fop[rows, :], samp[...], preferred_element_type=F32)

    load_samp.wait()
    load_fop[1].start()
    sib_send[0] = product(0)
    pl.semaphore_wait(barrier, len(peers))
    sib0 = go(remote(sib_send.at[0], sib_recv.at[0], sib_sem, (0,), sibling))
    acc[...] = product(1)
    sib0.wait_recv()

    def piece(d):
        return pl.ds(pl.multiple_of(((z + d) % 8) * UNIT, UNIT), UNIT)

    lanes = [pl.ds(pl.multiple_of(x_ * HALF, HALF), HALF) for x_ in (1 - xh, xh)]
    xs, zs, gz, gx = {}, {}, {}, {}

    def send_x(k):
        for d in FAR + (0,):
            x_send[k, d] = enc4(acc[piece(d), lanes[k]] + sib_recv[0, piece(d), lanes[k]])
            xs[k, d] = go(remote(x_send.at[k, d], x_recv.at[k, d], x_sem, (k, d), xpart))

    def send_z(k):
        for d in FAR:
            xs[k, d].wait_recv()
            z_send[k, d] = enc4(quad[piece(d), lanes[k]] + dec4(x_recv[k, d]))
            zs[k, d] = go(remote(z_send.at[k, d], z_recv.at[k, d], z_sem, (k, d), zpeer(d)))

    def unit_at(k, x_, z_):
        return sc_t.at[k, pl.ds(pl.multiple_of((core * 2 + x_) * BLK + z_ * UNIT, 16), UNIT)]

    def score(k):
        pred = quad[piece(0), lanes[k]]
        xs[k, 0].wait_recv()
        pred = pred + dec4(x_recv[k, 0])
        for d in FAR:
            zs[k, d].wait_recv()
            pred = pred + dec4(z_recv[k, d])
        error = obs_t[piece(0), lanes[k]] - pred
        unit_at(k, xl, z)[...] = student_score(error, prec_t[piece(0), :]).astype(BF16)

    def own_to(k, sem, d, device):
        return go(remote(unit_at(k, xl, z), unit_at(k, xl, z), sem, (k, d), device))

    def to_x(k, d):
        u = unit_at(k, xl, (z + 8 - d) % 8)
        return go(remote(u, u, gx_sem, (k, d), xpart))

    def gather(k):
        gx[k, 0] = to_x(k, 0)
        for d in RELAY + DIRECT:
            gz[k, d] = own_to(k, gz_sem, d, zpeer(d))
        for d in DIRECT:
            gx[k, d] = own_to(k, gx_sem, d, across(d))

    def relay(k):
        for d in RELAY:
            gz[k, d].wait_recv()
            gx[k, d] = to_x(k, d)
        for d in DIRECT:
            gz[k, d].wait_recv()

    def to_sibling(k, x_, i):
        b = sc_t.at[k, pl.ds(block_at(core, x_), BLK)]
        return go(remote(b, b, gs_sem, (k, i), sibling))

    def turn(k, c_, x_):
        b = pl.ds(block_at(c_, x_), BLK)
        sc[k, :, b] = sc_t[k, b, :].T

    def share_own(k):
        cp = to_sibling(k, xl, 0)
        turn(k, core, xl)
        return cp

    def share_other(k):
        for d in (0,) + DIRECT + RELAY:
            gx[k, d].wait_recv()
        cp = to_sibling(k, 1 - xl, 1)
        turn(k, core, 1 - xl)
        return cp

    def complete(k, first, second):
        first.wait_recv()
        turn(k, 1 - core, xl)
        second.wait_recv()
        turn(k, 1 - core, 1 - xl)

    send_x(0)
    send_x(1)
    sib_send[1] = product(2)
    sib1 = go(remote(sib_send.at[1], sib_recv.at[1], sib_sem, (1,), sibling))
    quad[...] = product(3)
    sib1.wait_recv()
    quad[...] = quad[...] + sib_recv[1]
    send_z(0)
    load_obs.wait()
    load_prec.wait()
    obs_t[...] = obs[...].T
    prec_t[...] = jnp.broadcast_to(prec[pl.ds(mine, BLK)].reshape(1, BLK), (HALF, BLK)).T
    send_z(1)
    score(0)
    gather(0)
    score(1)
    gather(1)
    relay(0)
    first0 = share_own(0)
    relay(1)
    second0 = share_other(0)
    complete(0, first0, second0)

    def columns(c):
        return pl.ds(pl.multiple_of(c * NC, NC), NC)

    def dest(y_):
        return pl.ds(pl.multiple_of(y_ * 32, 32), 32)

    def xx(i):
        return remote(xx_send.at[i], xx_recv.at[i], xx_sem, (i,), hpart)

    def xy(i, d):
        return remote(xy_send.at[i, d - 1], xy_recv.at[i, d - 1], xy_sem, (i, d - 1), ypeer(d))

    def yy(k, j, d):
        return remote(yy_send.at[k, j, d - 1], yy_recv.at[k, j, d - 1], yy_sem, (k, j, d - 1), ypeer(d))

    def yx(j):
        return remote(yx_send.at[j], yx_recv.at[j], yx_sem, (j,), hpart)

    def adjoint(k, c):
        return jnp.dot(sc[k], fop[:, columns(c)], preferred_element_type=F32)

    def x_other(i, c):
        xx_send[i] = enc2(adjoint(0, c))
        xx(i).start()

    def x_mine(i, c):
        parts[1, c] = adjoint(1, c)

    def y_part(k, j, c):
        parts[k, c] = adjoint(k, c)
        for d in (2, 1, 3):
            yy_send[k, j, d - 1] = enc2(parts[k, c, dest((y + d) % 4), :])
            yy(k, j, d).start()

    def y_other(j, c):
        y_part(0, j, c)

    def y_mine(j, c):
        y_part(1, j, c)

    def x_then_y(i, c):
        xx(i).wait_recv()
        for d in (2, 1, 3, 0):
            at = dest((y + d) % 4)
            v = parts[1, c, at, :] + dec2(xx_recv[i, at, :])
            if d:
                xy_send[i, d - 1] = enc2(v)
                xy(i, d).start()
            else:
                held[c] = v

    def y_total(k, j, c):
        v = parts[k, c, dest(y), :]
        for d in (1, 3, 2):
            yy(k, j, d).wait_recv()
            v = v + dec2(yy_recv[k, j, d - 1])
        return v

    def y_then_x(j, c):
        yx_send[j] = enc2(y_total(0, j, c))
        yx(j).start()

    def end_x_first(i, c):
        v = held[c]
        for d in (1, 3, 2):
            xy(i, d).wait_recv()
            v = v + dec2(xy_recv[i, d - 1])
        out_ref[:, columns(c)] = v

    def end_y_first(j, c):
        v = y_total(1, j, c)
        yx(j).wait_recv()
        out_ref[:, columns(c)] = v + dec2(yx_recv[j])

    def drain_x(i, c):
        xx(i).wait_send()
        for d in (1, 2, 3):
            xy(i, d).wait_send()

    def drain_y(j, c):
        yx(j).wait_send()
        for k in range(2):
            for d in (1, 2, 3):
                yy(k, j, d).wait_send()

    pairs = min(XF, YF)

    def sweep(on_x, on_y, lo=0, hi=CHUNKS):
        def both(t, carry):
            on_x(t, 2 * t)
            on_y(t, 2 * t + 1)
            return carry

        def rest(t, carry):
            (on_y if YF > XF else on_x)(t, t + pairs)
            return carry

        lax.fori_loop(lo, min(hi, pairs), both, 0)
        if hi > pairs and XF != YF:
            lax.fori_loop(max(lo, pairs), max(XF, YF), rest, 0)

    sweep(x_other, y_other, 0, EARLY)
    first1 = share_own(1)
    second1 = share_other(1)
    sweep(x_other, y_other, EARLY)
    complete(1, first1, second1)
    sweep(x_mine, y_mine)
    sweep(x_then_y, y_then_x)
    sweep(end_x_first, end_y_first)
    for cp in sends:
        cp.wait_send()
    sweep(drain_x, drain_y)


def local(forward_op, samples, observed, precision):
    dma = pltpu.SemaphoreType.DMA
    return pl.pallas_call(
        kernel,
        out_shape=jax.ShapeDtypeStruct((S // 8, NB), F32),
        in_specs=[pl.BlockSpec(memory_space=pltpu.HBM)] * 4,
        out_specs=pl.BlockSpec(memory_space=pltpu.VMEM),
        scratch_shapes=[
            pltpu.VMEM((MB, NB), BF16),
            pltpu.VMEM((NB, S), BF16),
            pltpu.VMEM((S, BLK), F32),
            pltpu.VMEM((MB,), F32),
            pltpu.VMEM((BLK, S), F32),
            pltpu.VMEM((BLK, 128), F32),
            pltpu.VMEM((2, BLK, S), F32),
            pltpu.VMEM((2, BLK, S), F32),
            pltpu.VMEM((BLK, S), F32),
            pltpu.VMEM((BLK, S), F32),
            pltpu.VMEM((2, 8, UNIT, HALF), BF16),
            pltpu.VMEM((2, 8, UNIT, HALF), BF16),
            pltpu.VMEM((2, 8, UNIT, HALF), BF16),
            pltpu.VMEM((2, 8, UNIT, HALF), BF16),
            pltpu.VMEM((2, MB, HALF), BF16),
            pltpu.VMEM((2, HALF, MB), BF16),
            pltpu.VMEM((2, CHUNKS, HALF, NC), F32),
            pltpu.VMEM((CHUNKS, 32, NC), F32),
            pltpu.VMEM((XF, HALF, NC), BF16),
            pltpu.VMEM((XF, HALF, NC), BF16),
            pltpu.VMEM((XF, 3, 32, NC), BF16),
            pltpu.VMEM((XF, 3, 32, NC), BF16),
            pltpu.VMEM((2, YF, 3, 32, NC), BF16),
            pltpu.VMEM((2, YF, 3, 32, NC), BF16),
            pltpu.VMEM((YF, 32, NC), BF16),
            pltpu.VMEM((YF, 32, NC), BF16),
            dma((7,)),
            dma((2, 2)),
            dma((2, 2, 8)),
            dma((2, 2, 8)),
            dma((2, 2, 8)),
            dma((2, 2, 8)),
            dma((2, 2, 2)),
            dma((2, XF)),
            dma((2, XF, 3)),
            dma((2, 2, YF, 3)),
            dma((2, YF)),
        ],
        compiler_params=pltpu.CompilerParams(
            collective_id=0, has_side_effects=True, vmem_limit_bytes=48 * 1024 * 1024
        ),
    )(*[pltpu.with_memory_space_constraint(a, pltpu.HBM) for a in (forward_op, samples, observed, precision)])


def solution(mesh):
    return jax.shard_map(
        local,
        mesh=mesh,
        in_specs=(P("row", "col"), P("col", None), P(None, "row"), P("row")),
        out_specs=P("row", "col"),
        check_vma=False,
    )
```

```python
import jax
import jax.numpy as jnp
from jax import lax
from jax.experimental import pallas as pl
from jax.experimental.pallas import tpu as pltpu
from jax.sharding import PartitionSpec as P

MESH = pl.DeviceIdType.MESH
F32 = jnp.float32
BF16 = jnp.bfloat16

S = 256
MB = 1536
NB = 3072
UNIT = 48
BLK = 384
NC = 512
CHUNKS = NB // NC
YF = 3
XF = CHUNKS - YF
HALF = 128
EARLY = 2
TINY = 1e-36
FAR = (4, 3, 5, 2, 6, 1, 7)
DIRECT = (1, 7, 2, 6)
RELAY = (4, 3, 5)
dof = 4.0


def enc4(v):
    w = v * v
    return (v * jnp.abs(v) * w).astype(BF16)


def dec4(c):
    v = c.astype(F32)
    t = lax.rsqrt(jnp.maximum(jnp.abs(v), TINY))
    return v * (t * t * lax.rsqrt(t))


def enc2(v):
    return (v * jnp.abs(v)).astype(BF16)


def dec2(c):
    v = c.astype(F32)
    return v * lax.rsqrt(jnp.maximum(jnp.abs(v), TINY))


def student_score(error, precision):
    return (dof + 1.0) * precision * error / (dof + precision * error * error)


def kernel(
    fop_hbm, samp_hbm, obs_hbm, prec_hbm, out_ref,
    fop, samp, obs, prec, obs_t, prec_t,
    sib_send, sib_recv, acc, quad, x_send, x_recv, z_send, z_recv,
    sc_t, sc, parts, held, xx_send, xx_recv, xy_send, xy_recv, yy_send, yy_recv, yx_send, yx_recv,
    load_sem, sib_sem, x_sem, z_sem, gz_sem, gx_sem, gs_sem, xx_sem, xy_sem, yy_sem, yx_sem,
):
    row = lax.axis_index("row")
    col = lax.axis_index("col")
    xh, y = row // 4, row % 4
    xl, z, core = col // 16, (col // 2) % 8, col % 2

    def at_col(x_, z_, c_):
        return (row, x_ * 16 + z_ * 2 + c_)

    sibling = at_col(xl, z, 1 - core)
    xpart = at_col(1 - xl, z, core)
    hpart = ((1 - xh) * 4 + y, col)

    def zpeer(d):
        return at_col(xl, (z + d) % 8, core)

    def across(d):
        return at_col(1 - xl, (z + d) % 8, core)

    def ypeer(d):
        return (xh * 4 + (y + d) % 4, col)

    def block_at(c_, x_):
        return pl.multiple_of((c_ * 2 + x_) * BLK, BLK)

    order = ((1 - core, 1 - xl), (core, 1 - xl), (1 - core, xl), (core, xl))
    mine = block_at(core, xl)

    load_samp = pltpu.make_async_copy(samp_hbm, samp, load_sem.at[4])
    load_fop = []
    for j, (c_, x_) in enumerate(order):
        rows = pl.ds(block_at(c_, x_), BLK)
        load_fop.append(pltpu.make_async_copy(fop_hbm.at[rows], fop.at[rows], load_sem.at[j]))
    load_obs = pltpu.make_async_copy(obs_hbm.at[:, pl.ds(mine, BLK)], obs, load_sem.at[5])
    load_prec = pltpu.make_async_copy(prec_hbm, prec, load_sem.at[6])
    load_samp.start()
    load_fop[0].start()

    barrier = pltpu.get_barrier_semaphore()
    peers = [sibling, xpart, hpart, ypeer(1), ypeer(2), ypeer(3)] + [zpeer(d) for d in range(1, 8)]
    peers += [across(d) for d in DIRECT]
    for p in peers:
        pl.semaphore_signal(barrier, inc=1, device_id=p, device_id_type=MESH)

    def remote(src, dst, sems, i, device):
        return pltpu.make_async_remote_copy(
            src_ref=src, dst_ref=dst, send_sem=sems.at[(0,) + i], recv_sem=sems.at[(1,) + i],
            device_id=device, device_id_type=MESH,
        )

    sends = []

    def go(cp):
        cp.start()
        sends.append(cp)
        return cp

    def product(j):
        load_fop[j].wait()
        if j < 2:
            load_fop[j + 2].start()
        if j == 1:
            load_obs.start()
            load_prec.start()
        rows = pl.ds(block_at(*order[j]), BLK)
        return jnp.dot(fop[rows, :], samp[...], preferred_element_type=F32)

    load_samp.wait()
    load_fop[1].start()
    sib_send[0] = product(0)
    pl.semaphore_wait(barrier, len(peers))
    sib0 = go(remote(sib_send.at[0], sib_recv.at[0], sib_sem, (0,), sibling))
    acc[...] = product(1)
    sib0.wait_recv()

    def piece(d):
        return pl.ds(pl.multiple_of(((z + d) % 8) * UNIT, UNIT), UNIT)

    lanes = [pl.ds(pl.multiple_of(x_ * HALF, HALF), HALF) for x_ in (1 - xh, xh)]
    xs, zs, gz, gx = {}, {}, {}, {}

    def send_x(k):
        for d in FAR + (0,):
            x_send[k, d] = enc4(acc[piece(d), lanes[k]] + sib_recv[0, piece(d), lanes[k]])
            xs[k, d] = go(remote(x_send.at[k, d], x_recv.at[k, d], x_sem, (k, d), xpart))

    def send_z(k):
        for d in FAR:
            xs[k, d].wait_recv()
            z_send[k, d] = enc4(quad[piece(d), lanes[k]] + dec4(x_recv[k, d]))
            zs[k, d] = go(remote(z_send.at[k, d], z_recv.at[k, d], z_sem, (k, d), zpeer(d)))

    def unit_at(k, x_, z_):
        return sc_t.at[k, pl.ds(pl.multiple_of((core * 2 + x_) * BLK + z_ * UNIT, 16), UNIT)]

    def score(k):
        pred = quad[piece(0), lanes[k]]
        xs[k, 0].wait_recv()
        pred = pred + dec4(x_recv[k, 0])
        for d in FAR:
            zs[k, d].wait_recv()
            pred = pred + dec4(z_recv[k, d])
        error = obs_t[piece(0), lanes[k]] - pred
        unit_at(k, xl, z)[...] = student_score(error, prec_t[piece(0), :]).astype(BF16)

    def own_to(k, sem, d, device):
        return go(remote(unit_at(k, xl, z), unit_at(k, xl, z), sem, (k, d), device))

    def to_x(k, d):
        u = unit_at(k, xl, (z + 8 - d) % 8)
        return go(remote(u, u, gx_sem, (k, d), xpart))

    def gather(k):
        gx[k, 0] = to_x(k, 0)
        for d in RELAY + DIRECT:
            gz[k, d] = own_to(k, gz_sem, d, zpeer(d))
        for d in DIRECT:
            gx[k, d] = own_to(k, gx_sem, d, across(d))

    def relay(k):
        for d in RELAY:
            gz[k, d].wait_recv()
            gx[k, d] = to_x(k, d)
        for d in DIRECT:
            gz[k, d].wait_recv()

    def to_sibling(k, x_, i):
        b = sc_t.at[k, pl.ds(block_at(core, x_), BLK)]
        return go(remote(b, b, gs_sem, (k, i), sibling))

    def turn(k, c_, x_):
        b = pl.ds(block_at(c_, x_), BLK)
        sc[k, :, b] = sc_t[k, b, :].T

    def share_own(k):
        cp = to_sibling(k, xl, 0)
        turn(k, core, xl)
        return cp

    def share_other(k):
        for d in (0,) + DIRECT + RELAY:
            gx[k, d].wait_recv()
        cp = to_sibling(k, 1 - xl, 1)
        turn(k, core, 1 - xl)
        return cp

    def complete(k, first, second):
        first.wait_recv()
        turn(k, 1 - core, xl)
        second.wait_recv()
        turn(k, 1 - core, 1 - xl)

    send_x(0)
    send_x(1)
    sib_send[1] = product(2)
    sib1 = go(remote(sib_send.at[1], sib_recv.at[1], sib_sem, (1,), sibling))
    quad[...] = product(3)
    sib1.wait_recv()
    quad[...] = quad[...] + sib_recv[1]
    send_z(0)
    load_obs.wait()
    load_prec.wait()
    obs_t[...] = obs[...].T
    prec_t[...] = jnp.broadcast_to(prec[pl.ds(mine, BLK)].reshape(1, BLK), (HALF, BLK)).T
    send_z(1)
    score(0)
    gather(0)
    score(1)
    gather(1)
    relay(0)
    first0 = share_own(0)
    relay(1)
    second0 = share_other(0)
    complete(0, first0, second0)

    def columns(c):
        return pl.ds(pl.multiple_of(c * NC, NC), NC)

    def dest(y_):
        return pl.ds(pl.multiple_of(y_ * 32, 32), 32)

    def xx(i):
        return remote(xx_send.at[i], xx_recv.at[i], xx_sem, (i,), hpart)

    def xy(i, d):
        return remote(xy_send.at[i, d - 1], xy_recv.at[i, d - 1], xy_sem, (i, d - 1), ypeer(d))

    def yy(k, j, d):
        return remote(yy_send.at[k, j, d - 1], yy_recv.at[k, j, d - 1], yy_sem, (k, j, d - 1), ypeer(d))

    def yx(j):
        return remote(yx_send.at[j], yx_recv.at[j], yx_sem, (j,), hpart)

    def adjoint(k, c):
        return jnp.dot(sc[k], fop[:, columns(c)], preferred_element_type=F32)

    def x_other(i, c):
        xx_send[i] = enc2(adjoint(0, c))
        xx(i).start()

    def x_mine(i, c):
        parts[1, c] = adjoint(1, c)

    def y_part(k, j, c):
        parts[k, c] = adjoint(k, c)
        for d in (2, 1, 3):
            yy_send[k, j, d - 1] = enc2(parts[k, c, dest((y + d) % 4), :])
            yy(k, j, d).start()

    def y_other(j, c):
        y_part(0, j, c)

    def y_mine(j, c):
        y_part(1, j, c)

    def x_then_y(i, c):
        xx(i).wait_recv()
        for d in (2, 1, 3, 0):
            at = dest((y + d) % 4)
            v = parts[1, c, at, :] + dec2(xx_recv[i, at, :])
            if d:
                xy_send[i, d - 1] = enc2(v)
                xy(i, d).start()
            else:
                held[c] = v

    def y_total(k, j, c):
        v = parts[k, c, dest(y), :]
        for d in (1, 3, 2):
            yy(k, j, d).wait_recv()
            v = v + dec2(yy_recv[k, j, d - 1])
        return v

    def y_then_x(j, c):
        yx_send[j] = enc2(y_total(0, j, c))
        yx(j).start()

    def end_x_first(i, c):
        v = held[c]
        for d in (1, 3, 2):
            xy(i, d).wait_recv()
            v = v + dec2(xy_recv[i, d - 1])
        out_ref[:, columns(c)] = v

    def end_y_first(j, c):
        v = y_total(1, j, c)
        yx(j).wait_recv()
        out_ref[:, columns(c)] = v + dec2(yx_recv[j])

    def sent_x(i, c):
        xx(i).wait_send()

    def drain_x(i, c):
        for d in (1, 2, 3):
            xy(i, d).wait_send()

    def sent_y(j, c):
        for k in range(2):
            for d in (1, 2, 3):
                yy(k, j, d).wait_send()

    def drain_y(j, c):
        yx(j).wait_send()

    pairs = min(XF, YF)

    def sweep(on_x, on_y, lo=0, hi=CHUNKS):
        def both(t, carry):
            on_x(t, 2 * t)
            on_y(t, 2 * t + 1)
            return carry

        def rest(t, carry):
            (on_y if YF > XF else on_x)(t, t + pairs)
            return carry

        lax.fori_loop(lo, min(hi, pairs), both, 0)
        if hi > pairs and XF != YF:
            lax.fori_loop(max(lo, pairs), max(XF, YF), rest, 0)

    sweep(x_other, y_other, 0, EARLY)
    first1 = share_own(1)
    second1 = share_other(1)
    sweep(x_other, y_other, EARLY)
    complete(1, first1, second1)
    sweep(x_mine, y_mine)
    for cp in sends:
        cp.wait_send()
    sweep(x_then_y, y_then_x)
    sweep(sent_x, sent_y)
    sweep(end_x_first, end_y_first)
    sweep(drain_x, drain_y)


def local(forward_op, samples, observed, precision):
    dma = pltpu.SemaphoreType.DMA
    return pl.pallas_call(
        kernel,
        out_shape=jax.ShapeDtypeStruct((S // 8, NB), F32),
        in_specs=[pl.BlockSpec(memory_space=pltpu.HBM)] * 4,
        out_specs=pl.BlockSpec(memory_space=pltpu.VMEM),
        scratch_shapes=[
            pltpu.VMEM((MB, NB), BF16),
            pltpu.VMEM((NB, S), BF16),
            pltpu.VMEM((S, BLK), F32),
            pltpu.VMEM((MB,), F32),
            pltpu.VMEM((BLK, S), F32),
            pltpu.VMEM((BLK, 128), F32),
            pltpu.VMEM((2, BLK, S), F32),
            pltpu.VMEM((2, BLK, S), F32),
            pltpu.VMEM((BLK, S), F32),
            pltpu.VMEM((BLK, S), F32),
            pltpu.VMEM((2, 8, UNIT, HALF), BF16),
            pltpu.VMEM((2, 8, UNIT, HALF), BF16),
            pltpu.VMEM((2, 8, UNIT, HALF), BF16),
            pltpu.VMEM((2, 8, UNIT, HALF), BF16),
            pltpu.VMEM((2, MB, HALF), BF16),
            pltpu.VMEM((2, HALF, MB), BF16),
            pltpu.VMEM((2, CHUNKS, HALF, NC), F32),
            pltpu.VMEM((CHUNKS, 32, NC), F32),
            pltpu.VMEM((XF, HALF, NC), BF16),
            pltpu.VMEM((XF, HALF, NC), BF16),
            pltpu.VMEM((XF, 3, 32, NC), BF16),
            pltpu.VMEM((XF, 3, 32, NC), BF16),
            pltpu.VMEM((2, YF, 3, 32, NC), BF16),
            pltpu.VMEM((2, YF, 3, 32, NC), BF16),
            pltpu.VMEM((YF, 32, NC), BF16),
            pltpu.VMEM((YF, 32, NC), BF16),
            dma((7,)),
            dma((2, 2)),
            dma((2, 2, 8)),
            dma((2, 2, 8)),
            dma((2, 2, 8)),
            dma((2, 2, 8)),
            dma((2, 2, 2)),
            dma((2, XF)),
            dma((2, XF, 3)),
            dma((2, 2, YF, 3)),
            dma((2, YF)),
        ],
        compiler_params=pltpu.CompilerParams(
            collective_id=0, has_side_effects=True, vmem_limit_bytes=48 * 1024 * 1024
        ),
    )(*[pltpu.with_memory_space_constraint(a, pltpu.HBM) for a in (forward_op, samples, observed, precision)])


def solution(mesh):
    return jax.shard_map(
        local,
        mesh=mesh,
        in_specs=(P("row", "col"), P("col", None), P(None, "row"), P("row")),
        out_specs=P("row", "col"),
        check_vma=False,
    )
```
